32 devices in a mesh: section: 4 (over y, x), scen: 8 (over z, core).
Axes of the slice: x: 2, y: 2, z: 4, core: 2. Of those that a mesh axis runs over, the one named last changes fastest.
Arguments:
- right_side: float32 [4, 8, 512, 1024], P('section', 'scen'), may hold values from -6 to 6
- inverse_raw: bfloat16 [4, 8, 1024, 1024], P('section', 'scen'), may hold values from -0.1875 to 0.1875
- inverse_pattern: int32 [4, 8, 16, 16], P('section', 'scen'), may hold values 0 or 1
- coupling: bfloat16 [4, 8, 1024, 1024], P('section', 'scen'), may hold values from -0.1875 to 0.1875
- coupling_pattern: int32 [4, 8, 16, 16], P('section', 'scen'), may hold values 0 or 1
- pivots: float32 [4, 8, 1024], P('section', 'scen'), may hold values from 0.5 to 2
- offsets: int32 [4, 8], replicated, may hold values from 0 to 1, as said below
- above_solution: bfloat16 [8, 512, 1024], P('scen'), may hold values from -6 to 6
Outputs:
- solution: float32 [4, 8, 512, 1024], P('section', 'scen')
The draws below stay inside these ranges and needn't reach their ends.
Inputs may be any that keep to these rules, and one draw needn't show every extreme that they name: Node c of level l has node c + offsets[l, c] of level l - 1 as its parent, and for l = 0 row c + offsets[0, c] of above_solution; offsets[l, 0] is 1 and offsets[l, 7] is 0 for every l.
All inputs are finite; a program needn't handle non-finite values. No bound on the sum of `inverse_pattern` or of `coupling_pattern` on one device may be relied on, other than what follows from the above.
Results may differ from the reference program's by a relative error of at most 0.0075.
Values may be sent and summed in bfloat16 or wider, within the bound.
A program may use at most 64 MiB of HBM per device.

```python
import math
import jax
import jax.numpy as jnp
from jax import lax

NA = 1024
NB = 16
COLS = 512
LEVELS = 4
NODES = 8


def draw_offsets(key, part):
    picked = jax.random.randint(key, (LEVELS, NODES), 0, 2)
    col_ids = jnp.arange(NODES)[None, :]
    middle = NODES // 2
    picked = jnp.where((col_ids >= middle - 2) & (col_ids <= middle), 1, picked)
    picked = jnp.where(col_ids == 0, 1, picked)
    return jnp.where(col_ids == NODES - 1, 0, picked).astype(jnp.int32)


def set_ends(values, stream_key, least, high):
    longest = values.shape.index(max(values.shape))
    spots = []
    for shift in (0, 1):
        where = [jax.random.randint(jax.random.fold_in(stream_key, axis), (), 0, length) for axis, length in enumerate(values.shape)]
        where[longest] = (where[longest] + shift) % values.shape[longest]
        spots.append(tuple(where))
    return values.at[spots[0]].set(least).at[spots[1]].set(high)


def block_levels(rng, extent, pieces, low, largest):
    level = 1.0
    for position, shards_of in pieces:
        steps = jax.random.uniform(jax.random.fold_in(jax.random.fold_in(rng, 6), position), (shards_of,), jnp.float32, low / len(pieces), largest / len(pieces))
        level = level * jnp.repeat(jnp.exp(steps), extent[position] // shards_of).reshape((-1,) + (1,) * (len(extent) - 1 - position))
    return level


def noise(own_key, shape, scale, most, pieces=(), dtype=jnp.bfloat16):
    entries = scale * jax.random.normal(own_key, shape, jnp.float32)
    if pieces:
        entries = entries * block_levels(own_key, shape, pieces, -0.22, 0.18)
    return jnp.clip(entries, -most, most).astype(dtype)


def setup_inputs(seed: int = 0) -> dict:
    key_of = jax.random.split(jax.random.key(seed), 9)
    right_side = noise(key_of[0], (LEVELS, NODES, COLS, NA), 1.0, 6.0, ((0, 4), (1, 8)), jnp.float32)
    inverse_raw = noise(key_of[1], (LEVELS, NODES, NA, NA), NA ** -0.5, 0.1875, ((0, 4), (1, 8)))
    inverse_pattern = set_ends((jax.random.randint(key_of[2], (LEVELS, NODES, NB, NB), 0, 2) < 1).astype(jnp.int32), jax.random.fold_in(key_of[2], 1), 0, 1)
    coupling = noise(key_of[3], (LEVELS, NODES, NA, NA), NA ** -0.5, 0.1875, ((0, 4), (1, 8)))
    coupling_pattern = set_ends((jax.random.randint(key_of[4], (LEVELS, NODES, NB, NB), 0, 2) < 1).astype(jnp.int32), jax.random.fold_in(key_of[4], 1), 0, 1)
    pivots = jnp.clip(jnp.exp(math.log(2.0) - 1.3862944 * jax.random.uniform(key_of[5], (LEVELS, NODES, NA), jnp.float32) ** block_levels(key_of[5], (LEVELS, NODES, NA), ((0, 4), (1, 8)), -0.2, 0.2)), 0.5, 2.0)
    offsets = draw_offsets(jax.random.fold_in(key_of[8], 71), 0)
    above_solution = noise(key_of[7], (NODES, COLS, NA), 1.0, 6.0, ((0, 8),))
    return dict(right_side=right_side, inverse_raw=inverse_raw, inverse_pattern=inverse_pattern, coupling=coupling, coupling_pattern=coupling_pattern, pivots=pivots, offsets=offsets, above_solution=above_solution)


def times_transposed(left_rows, matrix):
    return lax.dot_general(left_rows, matrix, (((1,), (1,)), ((), ())), preferred_element_type=jnp.float32)


def widen_pattern(pattern, block_size):
    return jnp.repeat(jnp.repeat(pattern, block_size, axis=0), block_size, axis=1)


def unit_inverse(raw_values, pattern):
    features = raw_values.shape[0]
    widened = widen_pattern(pattern, features // pattern.shape[0])
    row_ids = lax.broadcasted_iota(jnp.int32, (features, features), 0)
    col_ids = lax.broadcasted_iota(jnp.int32, (features, features), 1)
    kept_mask = (widened > 0) & (row_ids > col_ids)
    unit_part = jnp.where(row_ids == col_ids, jnp.ones_like(raw_values), jnp.zeros_like(raw_values))
    return jnp.where(kept_mask, raw_values, unit_part)


def masked_coupling(raw_values, pattern):
    widened = widen_pattern(pattern, raw_values.shape[0] // pattern.shape[0])
    return jnp.where(widened > 0, raw_values, jnp.zeros_like(raw_values))


def forward_node(packed):
    given, arriving, raw_values, pattern, link_raw, link_pattern, pivot_row = packed
    factor = unit_inverse(raw_values, pattern)
    linking = masked_coupling(link_raw, link_pattern)
    forward_rows = times_transposed((given - arriving).astype(jnp.bfloat16), factor)
    child_term = times_transposed(forward_rows.astype(jnp.bfloat16), linking).astype(jnp.bfloat16)
    return forward_rows * pivot_row[None, :], child_term


def backward_node(packed):
    weighted, parent_rows, raw_values, pattern, link_raw, link_pattern = packed
    factor = unit_inverse(raw_values, pattern)
    linking = masked_coupling(link_raw, link_pattern)
    reduced = weighted - jnp.dot(parent_rows, linking, preferred_element_type=jnp.float32)
    return jnp.dot(reduced.astype(jnp.bfloat16), factor, preferred_element_type=jnp.float32)


def reference(right_side, inverse_raw, inverse_pattern, coupling, coupling_pattern, pivots, offsets, above_solution):
    incoming = jnp.zeros(right_side.shape[1:], jnp.float32)
    kept_levels = []
    for level_index in range(LEVELS - 1, -1, -1):
        weighted, child_term = lax.map(forward_node, (right_side[level_index], incoming, inverse_raw[level_index], inverse_pattern[level_index], coupling[level_index], coupling_pattern[level_index], pivots[level_index]))
        kept_levels.insert(0, weighted)
        offset_row = offsets[level_index][:, None, None]
        terms_wide = child_term.astype(jnp.float32)
        own_terms = jnp.where(offset_row == 0, terms_wide, 0.0)
        moved_terms = jnp.where(offset_row == 1, terms_wide, 0.0)
        incoming = own_terms + jnp.concatenate([jnp.zeros_like(moved_terms[:1]), moved_terms[:-1]], axis=0)
    upper_rows = above_solution
    solutions = []
    for level_index in range(LEVELS):
        offset_row = offsets[level_index][:, None, None]
        next_upper = jnp.concatenate([upper_rows[1:], jnp.zeros_like(upper_rows[:1])], axis=0)
        parent_rows = jnp.where(offset_row == 1, next_upper, upper_rows)
        solved = lax.map(backward_node, (kept_levels[level_index], parent_rows, inverse_raw[level_index], inverse_pattern[level_index], coupling[level_index], coupling_pattern[level_index]))
        solutions.append(solved)
        upper_rows = solved.astype(jnp.bfloat16)
    return jnp.stack(solutions, axis=0)
```

```python
import functools

import jax
import jax.numpy as jnp
from jax import lax
from jax.experimental import pallas as pl
from jax.experimental.pallas import tpu as pltpu
from jax.sharding import PartitionSpec as P

ROWS = 64
LAG = 4
TILE = 256
MESH = pl.DeviceIdType.MESH


def dot_nt(a, b):
    return lax.dot_general(a, b, (((1,), (1,)), ((), ())), preferred_element_type=jnp.float32)


def dot_nn(a, b):
    return lax.dot_general(a, b, (((1,), (0,)), ((), ())), preferred_element_type=jnp.float32)


def kernel(
    levels,
    nodes,
    rows,
    given_ref,
    raw_ref,
    pattern_ref,
    coupling_ref,
    coupling_pattern_ref,
    pivot_ref,
    offsets_ref,
    above_ref,
    out_ref,
    factor,
    link,
    kept,
    up_in,
    up_out,
    side_in,
    side_out,
    dside_in,
    dside_out,
    down_in,
    down_out,
    above_side,
    up_sems,
    side_sems,
    dside_sems,
    down_sems,
    above_sems,
):
    s = lax.axis_index("section")
    j = lax.axis_index("scen")
    total, features = given_ref.shape
    pieces = total // rows
    blocks = pattern_ref.shape[0]
    size = features // blocks
    has_up, has_down = s > 0, s < levels - 1
    has_left, has_right = j > 0, j < nodes - 1
    up_id = {"section": lax.rem(s + levels - 1, levels)}
    down_id = {"section": lax.rem(s + 1, levels)}
    right_id = {"scen": lax.rem(j + 1, nodes)}
    left_id = {"scen": lax.rem(j + nodes - 1, nodes)}

    barrier = pltpu.get_barrier_semaphore()
    count = jnp.int32(0)
    for has, where_to in ((has_up, up_id), (has_down, down_id), (has_left, left_id), (has_right, right_id)):

        @pl.when(has)
        def _(where_to=where_to):
            pl.semaphore_signal(barrier, inc=1, device_id=where_to, device_id_type=MESH)

        count = count + has.astype(jnp.int32)
    pl.semaphore_wait(barrier, count)

    def slot(ref, p):
        return ref.at[pl.ds(pl.multiple_of(p * rows, rows), rows), :]

    def copy(src, dst, sems, p, device):
        return pltpu.make_async_remote_copy(
            src_ref=slot(src, p),
            dst_ref=slot(dst, p),
            send_sem=sems.at[0, p],
            recv_sem=sems.at[1, p],
            device_id=device,
            device_id_type=MESH,
        )

    def up_copy(p):
        return copy(up_out, up_in, up_sems, p, up_id)

    def side_copy(p):
        return copy(side_out, side_in, side_sems, p, right_id)

    def dside_copy(p):
        return copy(dside_out, dside_in, dside_sems, p, left_id)

    def down_copy(p):
        return copy(down_out, down_in, down_sems, p, down_id)

    def above_copy():
        return pltpu.make_async_remote_copy(
            src_ref=above_ref,
            dst_ref=above_side,
            send_sem=above_sems.at[0],
            recv_sem=above_sems.at[1],
            device_id=left_id,
            device_id_type=MESH,
        )

    first = s == 0

    @pl.when(first & has_left)
    def _():
        above_copy().start()

    @pl.when(jnp.logical_not(has_down))
    def _():
        up_in[...] = jnp.zeros_like(up_in)

    @pl.when(jnp.logical_not(has_left))
    def _():
        side_in[...] = jnp.zeros_like(side_in)

    @pl.when(jnp.logical_not(has_right))
    def _():
        dside_in[...] = jnp.zeros_like(dside_in)
        above_side[...] = jnp.zeros_like(above_side)

    spread = (
        lax.broadcasted_iota(jnp.int32, (blocks, features), 1) // size
        == lax.broadcasted_iota(jnp.int32, (blocks, features), 0)
    ).astype(jnp.bfloat16)
    factor_mask = dot_nn(pattern_ref[...].astype(jnp.float32).astype(jnp.bfloat16), spread)
    link_mask = dot_nn(coupling_pattern_ref[...].astype(jnp.float32).astype(jnp.bfloat16), spread)
    col_ids = lax.broadcasted_iota(jnp.int32, (size, features), 1)
    for i in range(blocks):
        part = pl.ds(i * size, size)
        row_ids = lax.broadcasted_iota(jnp.int32, (size, features), 0) + i * size
        keep = (factor_mask[i : i + 1, :] > 0.5) & (row_ids > col_ids)
        unit = jnp.where(row_ids == col_ids, 1.0, 0.0)
        factor[part, :] = jnp.where(keep, raw_ref[part, :].astype(jnp.float32), unit).astype(jnp.bfloat16)
        link[part, :] = jnp.where(
            link_mask[i : i + 1, :] > 0.5, coupling_ref[part, :].astype(jnp.float32), 0.0
        ).astype(jnp.bfloat16)

    own_offset = offsets_ref[s, j]
    left_offset = offsets_ref[s, jnp.maximum(j - 1, 0)]
    child_offset = offsets_ref[jnp.minimum(s + 1, levels - 1), j]
    tile = min(TILE, features)

    def forward(p):
        @pl.when(has_down)
        def _():
            up_copy(p).wait_recv()

        here = pl.ds(pl.multiple_of(p * rows, rows), rows)
        reduced = (given_ref[here, :] - up_in[here, :].astype(jnp.float32)).astype(jnp.bfloat16)
        result = jnp.concatenate(
            [
                dot_nt(reduced[:, : n + tile], factor[n : n + tile, : n + tile])
                for n in range(0, features, tile)
            ],
            axis=1,
        )
        kept[here, :] = result * pivot_ref[...]

        @pl.when(has_up)
        def _():
            side_out[here, :] = dot_nt(result.astype(jnp.bfloat16), link[...]).astype(jnp.bfloat16)

            @pl.when(has_right)
            def _():
                side_copy(p).start()

    def combine(p):
        @pl.when(has_up)
        def _():
            @pl.when(has_left)
            def _():
                side_copy(p).wait_recv()

            here = pl.ds(pl.multiple_of(p * rows, rows), rows)
            own = jnp.where(own_offset == 0, side_out[here, :].astype(jnp.float32), 0.0)
            moved = jnp.where(left_offset == 1, side_in[here, :].astype(jnp.float32), 0.0)
            up_out[here, :] = (own + jnp.where(has_left, moved, 0.0)).astype(jnp.bfloat16)
            up_copy(p).start()

    def backward(p):
        @pl.when(has_up)
        def _():
            down_copy(p).wait_recv()

        here = pl.ds(pl.multiple_of(p * rows, rows), rows)
        reduced = (kept[here, :] - dot_nn(down_in[here, :], link[...])).astype(jnp.bfloat16)
        result = jnp.concatenate(
            [dot_nn(reduced[:, n:], factor[n:, n : n + tile]) for n in range(0, features, tile)], axis=1
        )
        out_ref[here, :] = result

        @pl.when(has_down)
        def _():
            dside_out[here, :] = result.astype(jnp.bfloat16)

            @pl.when(has_left)
            def _():
                dside_copy(p).start()

    def select(p):
        @pl.when(has_down)
        def _():
            @pl.when(has_right)
            def _():
                dside_copy(p).wait_recv()

            here = pl.ds(pl.multiple_of(p * rows, rows), rows)
            down_out[here, :] = jnp.where(
                child_offset == 1,
                dside_in[here, :].astype(jnp.float32),
                dside_out[here, :].astype(jnp.float32),
            ).astype(jnp.bfloat16)
            down_copy(p).start()

    @pl.when(first)
    def _():
        @pl.when(has_right)
        def _():
            above_copy().wait_recv()

        down_in[...] = jnp.where(
            own_offset == 1, above_side[...].astype(jnp.float32), above_ref[...].astype(jnp.float32)
        ).astype(jnp.bfloat16)

    lag = jnp.minimum(LAG * s, pieces)

    def turn(u, carry):
        @pl.when(u < pieces)
        def _():
            forward(u)

        @pl.when((u >= 1) & (u <= pieces))
        def _():
            combine(u - 1)

        v = u - lag

        @pl.when((v >= 0) & (v < pieces))
        def _():
            backward(v)

        @pl.when((v >= 1) & (v <= pieces))
        def _():
            select(v - 1)

        return carry

    lax.fori_loop(0, pieces + lag + 1, turn, 0)

    def finish(p, carry):
        @pl.when(has_up)
        def _():
            up_copy(p).wait_send()

            @pl.when(has_right)
            def _():
                side_copy(p).wait_send()

        @pl.when(has_down)
        def _():
            down_copy(p).wait_send()

            @pl.when(has_left)
            def _():
                dside_copy(p).wait_send()

        return carry

    lax.fori_loop(0, pieces, finish, 0)

    @pl.when(first & has_left)
    def _():
        above_copy().wait_send()


def local(
    right_side,
    inverse_raw,
    inverse_pattern,
    coupling,
    coupling_pattern,
    pivots,
    offsets,
    above_solution,
):
    levels = lax.axis_size("section")
    nodes = lax.axis_size("scen")
    total, features = right_side.shape[2:]
    rows = min(ROWS, total)
    pieces = total // rows
    vmem = pl.BlockSpec(memory_space=pltpu.VMEM)
    half = pltpu.VMEM((total, features), jnp.bfloat16)
    square = pltpu.VMEM((features, features), jnp.bfloat16)
    sems = pltpu.SemaphoreType.DMA((2, pieces))
    solved = pl.pallas_call(
        functools.partial(kernel, levels, nodes, rows),
        out_shape=jax.ShapeDtypeStruct((total, features), jnp.float32),
        in_specs=[vmem] * 6 + [pl.BlockSpec(memory_space=pltpu.SMEM), vmem],
        out_specs=vmem,
        scratch_shapes=[square, square, pltpu.VMEM((total, features), jnp.float32)]
        + [half] * 9
        + [sems] * 4
        + [pltpu.SemaphoreType.DMA((2,))],
        compiler_params=pltpu.CompilerParams(
            collective_id=0, has_side_effects=True, vmem_limit_bytes=60 * 1024 * 1024
        ),
    )(
        right_side[0, 0],
        inverse_raw[0, 0],
        inverse_pattern[0, 0],
        coupling[0, 0],
        coupling_pattern[0, 0],
        pivots[0],
        offsets,
        above_solution[0],
    )
    return solved[None, None]


def solution(mesh):
    placed = (
        P("section", "scen", None, None),
        P("section", "scen", None, None),
        P("section", "scen", None, None),
        P("section", "scen", None, None),
        P("section", "scen", None, None),
        P("section", "scen", None),
        P(),
        P("scen", None, None),
    )
    return jax.shard_map(
        local,
        mesh=mesh,
        in_specs=placed,
        out_specs=P("section", "scen", None, None),
        check_vma=False,
    )
```

```python
import functools

import jax
import jax.numpy as jnp
from jax import lax
from jax.experimental import pallas as pl
from jax.experimental.pallas import tpu as pltpu
from jax.sharding import PartitionSpec as P

ROWS = 32
LAG = 8
TILE = 256
MESH = pl.DeviceIdType.MESH


def dot_nt(a, b):
    return lax.dot_general(a, b, (((1,), (1,)), ((), ())), preferred_element_type=jnp.float32)


def dot_nn(a, b):
    return lax.dot_general(a, b, (((1,), (0,)), ((), ())), preferred_element_type=jnp.float32)


def kernel(
    levels,
    nodes,
    rows,
    given_ref,
    raw_ref,
    pattern_ref,
    coupling_ref,
    coupling_pattern_ref,
    pivot_ref,
    offsets_ref,
    above_ref,
    out_ref,
    factor,
    link,
    kept,
    up_in,
    up_out,
    side_in,
    side_out,
    dside_in,
    dside_out,
    down_in,
    down_out,
    above_side,
    up_sems,
    side_sems,
    dside_sems,
    down_sems,
    above_sems,
):
    s = lax.axis_index("section")
    j = lax.axis_index("scen")
    total, features = given_ref.shape
    pieces = total // rows
    blocks = pattern_ref.shape[0]
    size = features // blocks
    has_up, has_down = s > 0, s < levels - 1
    has_left, has_right = j > 0, j < nodes - 1
    up_id = {"section": lax.rem(s + levels - 1, levels)}
    down_id = {"section": lax.rem(s + 1, levels)}
    right_id = {"scen": lax.rem(j + 1, nodes)}
    left_id = {"scen": lax.rem(j + nodes - 1, nodes)}

    barrier = pltpu.get_barrier_semaphore()
    count = jnp.int32(0)
    for has, where_to in ((has_up, up_id), (has_down, down_id), (has_left, left_id), (has_right, right_id)):

        @pl.when(has)
        def _(where_to=where_to):
            pl.semaphore_signal(barrier, inc=1, device_id=where_to, device_id_type=MESH)

        count = count + has.astype(jnp.int32)
    pl.semaphore_wait(barrier, count)

    def slot(ref, p):
        return ref.at[pl.ds(pl.multiple_of(p * rows, rows), rows), :]

    def copy(src, dst, sems, p, device):
        return pltpu.make_async_remote_copy(
            src_ref=slot(src, p),
            dst_ref=slot(dst, p),
            send_sem=sems.at[0, p],
            recv_sem=sems.at[1, p],
            device_id=device,
            device_id_type=MESH,
        )

    def up_copy(p):
        return copy(up_out, up_in, up_sems, p, up_id)

    def side_copy(p):
        return copy(side_out, side_in, side_sems, p, right_id)

    def dside_copy(p):
        return copy(dside_out, dside_in, dside_sems, p, left_id)

    def down_copy(p):
        return copy(down_out, down_in, down_sems, p, down_id)

    def above_copy():
        return pltpu.make_async_remote_copy(
            src_ref=above_ref,
            dst_ref=above_side,
            send_sem=above_sems.at[0],
            recv_sem=above_sems.at[1],
            device_id=left_id,
            device_id_type=MESH,
        )

    first = s == 0

    @pl.when(first & has_left)
    def _():
        above_copy().start()

    @pl.when(jnp.logical_not(has_down))
    def _():
        up_in[...] = jnp.zeros_like(up_in)

    @pl.when(jnp.logical_not(has_left))
    def _():
        side_in[...] = jnp.zeros_like(side_in)

    @pl.when(jnp.logical_not(has_right))
    def _():
        dside_in[...] = jnp.zeros_like(dside_in)
        above_side[...] = jnp.zeros_like(above_side)

    spread = (
        lax.broadcasted_iota(jnp.int32, (blocks, features), 1) // size
        == lax.broadcasted_iota(jnp.int32, (blocks, features), 0)
    ).astype(jnp.bfloat16)
    factor_mask = dot_nn(pattern_ref[...].astype(jnp.float32).astype(jnp.bfloat16), spread)
    link_mask = dot_nn(coupling_pattern_ref[...].astype(jnp.float32).astype(jnp.bfloat16), spread)
    col_ids = lax.broadcasted_iota(jnp.int32, (size, features), 1)
    for i in range(blocks):
        part = pl.ds(i * size, size)
        row_ids = lax.broadcasted_iota(jnp.int32, (size, features), 0) + i * size
        keep = (factor_mask[i : i + 1, :] > 0.5) & (row_ids > col_ids)
        unit = jnp.where(row_ids == col_ids, 1.0, 0.0)
        factor[part, :] = jnp.where(keep, raw_ref[part, :].astype(jnp.float32), unit).astype(jnp.bfloat16)
        link[part, :] = jnp.where(
            link_mask[i : i + 1, :] > 0.5, coupling_ref[part, :].astype(jnp.float32), 0.0
        ).astype(jnp.bfloat16)

    own_offset = offsets_ref[s, j]
    left_offset = offsets_ref[s, jnp.maximum(j - 1, 0)]
    child_offset = offsets_ref[jnp.minimum(s + 1, levels - 1), j]
    tile = min(TILE, features)

    def forward(p):
        @pl.when(has_down)
        def _():
            up_copy(p).wait_recv()

        here = pl.ds(pl.multiple_of(p * rows, rows), rows)
        reduced = (given_ref[here, :] - up_in[here, :].astype(jnp.float32)).astype(jnp.bfloat16)
        result = jnp.concatenate(
            [
                dot_nt(reduced[:, : n + tile], factor[n : n + tile, : n + tile])
                for n in range(0, features, tile)
            ],
            axis=1,
        )
        kept[here, :] = result * pivot_ref[...]

        @pl.when(has_up)
        def _():
            side_out[here, :] = dot_nt(result.astype(jnp.bfloat16), link[...]).astype(jnp.bfloat16)

            @pl.when(has_right)
            def _():
                side_copy(p).start()

    def combine(p):
        @pl.when(has_up)
        def _():
            @pl.when(has_left)
            def _():
                side_copy(p).wait_recv()

            here = pl.ds(pl.multiple_of(p * rows, rows), rows)
            own = jnp.where(own_offset == 0, side_out[here, :].astype(jnp.float32), 0.0)
            moved = jnp.where(left_offset == 1, side_in[here, :].astype(jnp.float32), 0.0)
            up_out[here, :] = (own + jnp.where(has_left, moved, 0.0)).astype(jnp.bfloat16)
            up_copy(p).start()

    def backward(p):
        @pl.when(has_up)
        def _():
            down_copy(p).wait_recv()

        here = pl.ds(pl.multiple_of(p * rows, rows), rows)
        reduced = (kept[here, :] - dot_nn(down_in[here, :], link[...])).astype(jnp.bfloat16)
        result = jnp.concatenate(
            [dot_nn(reduced[:, n:], factor[n:, n : n + tile]) for n in range(0, features, tile)], axis=1
        )
        out_ref[here, :] = result

        @pl.when(has_down)
        def _():
            dside_out[here, :] = result.astype(jnp.bfloat16)

            @pl.when(has_left)
            def _():
                dside_copy(p).start()

    def select(p):
        @pl.when(has_down)
        def _():
            @pl.when(has_right)
            def _():
                dside_copy(p).wait_recv()

            here = pl.ds(pl.multiple_of(p * rows, rows), rows)
            down_out[here, :] = jnp.where(
                child_offset == 1,
                dside_in[here, :].astype(jnp.float32),
                dside_out[here, :].astype(jnp.float32),
            ).astype(jnp.bfloat16)
            down_copy(p).start()

    @pl.when(first)
    def _():
        @pl.when(has_right)
        def _():
            above_copy().wait_recv()

        down_in[...] = jnp.where(
            own_offset == 1, above_side[...].astype(jnp.float32), above_ref[...].astype(jnp.float32)
        ).astype(jnp.bfloat16)

    lag = jnp.minimum(LAG * s, pieces)

    def turn(u, carry):
        @pl.when(u < pieces)
        def _():
            forward(u)

        @pl.when((u >= 1) & (u <= pieces))
        def _():
            combine(u - 1)

        v = u - lag

        @pl.when((v >= 0) & (v < pieces))
        def _():
            backward(v)

        @pl.when((v >= 1) & (v <= pieces))
        def _():
            select(v - 1)

        return carry

    lax.fori_loop(0, pieces + lag + 1, turn, 0)

    def finish(p, carry):
        @pl.when(has_up)
        def _():
            up_copy(p).wait_send()

            @pl.when(has_right)
            def _():
                side_copy(p).wait_send()

        @pl.when(has_down)
        def _():
            down_copy(p).wait_send()

            @pl.when(has_left)
            def _():
                dside_copy(p).wait_send()

        return carry

    lax.fori_loop(0, pieces, finish, 0)

    @pl.when(first & has_left)
    def _():
        above_copy().wait_send()


def local(
    right_side,
    inverse_raw,
    inverse_pattern,
    coupling,
    coupling_pattern,
    pivots,
    offsets,
    above_solution,
):
    levels = lax.axis_size("section")
    nodes = lax.axis_size("scen")
    total, features = right_side.shape[2:]
    rows = min(ROWS, total)
    pieces = total // rows
    vmem = pl.BlockSpec(memory_space=pltpu.VMEM)
    half = pltpu.VMEM((total, features), jnp.bfloat16)
    square = pltpu.VMEM((features, features), jnp.bfloat16)
    sems = pltpu.SemaphoreType.DMA((2, pieces))
    solved = pl.pallas_call(
        functools.partial(kernel, levels, nodes, rows),
        out_shape=pltpu.VMEM((total, features), jnp.float32),
        in_specs=[vmem] * 6 + [pl.BlockSpec(memory_space=pltpu.SMEM), vmem],
        out_specs=vmem,
        scratch_shapes=[square, square, pltpu.VMEM((total, features), jnp.float32)]
        + [half] * 9
        + [sems] * 4
        + [pltpu.SemaphoreType.DMA((2,))],
        compiler_params=pltpu.CompilerParams(
            collective_id=0, has_side_effects=True, vmem_limit_bytes=60 * 1024 * 1024
        ),
    )(
        right_side[0, 0],
        inverse_raw[0, 0],
        inverse_pattern[0, 0],
        coupling[0, 0],
        coupling_pattern[0, 0],
        pivots[0],
        offsets,
        above_solution[0],
    )
    return solved[None, None]


def solution(mesh):
    placed = (
        P("section", "scen", None, None),
        P("section", "scen", None, None),
        P("section", "scen", None, None),
        P("section", "scen", None, None),
        P("section", "scen", None, None),
        P("section", "scen", None),
        P(),
        P("scen", None, None),
    )
    return jax.shard_map(
        local,
        mesh=mesh,
        in_specs=placed,
        out_specs=P("section", "scen", None, None),
        check_vma=False,
    )
```

```python
import functools

import jax
import jax.numpy as jnp
from jax import lax
from jax.experimental import pallas as pl
from jax.experimental.pallas import tpu as pltpu
from jax.sharding import PartitionSpec as P

ROWS = 32
LAG = 8
TILE = 256
MESH = pl.DeviceIdType.MESH


def dot_nn(a, b):
    return lax.dot_general(a, b, (((1,), (0,)), ((), ())), preferred_element_type=jnp.float32)


def kernel(
    levels,
    nodes,
    rows,
    given_ref,
    raw_ref,
    pattern_ref,
    coupling_ref,
    coupling_pattern_ref,
    pivot_ref,
    offsets_ref,
    above_ref,
    out_ref,
    factor,
    link,
    factor_t,
    link_t,
    kept,
    up_in,
    up_out,
    side_in,
    side_out,
    dside_in,
    dside_out,
    down_in,
    down_out,
    above_side,
    up_sems,
    side_sems,
    dside_sems,
    down_sems,
    above_sems,
):
    s = lax.axis_index("section")
    j = lax.axis_index("scen")
    total, features = given_ref.shape
    pieces = total // rows
    blocks = pattern_ref.shape[0]
    size = features // blocks
    has_up, has_down = s > 0, s < levels - 1
    has_left, has_right = j > 0, j < nodes - 1
    up_id = {"section": lax.rem(s + levels - 1, levels)}
    down_id = {"section": lax.rem(s + 1, levels)}
    right_id = {"scen": lax.rem(j + 1, nodes)}
    left_id = {"scen": lax.rem(j + nodes - 1, nodes)}

    barrier = pltpu.get_barrier_semaphore()
    count = jnp.int32(0)
    for has, where_to in ((has_up, up_id), (has_down, down_id), (has_left, left_id), (has_right, right_id)):

        @pl.when(has)
        def _(where_to=where_to):
            pl.semaphore_signal(barrier, inc=1, device_id=where_to, device_id_type=MESH)

        count = count + has.astype(jnp.int32)
    pl.semaphore_wait(barrier, count)

    def slot(ref, p):
        return ref.at[pl.ds(pl.multiple_of(p * rows, rows), rows), :]

    def copy(src, dst, sems, p, device):
        return pltpu.make_async_remote_copy(
            src_ref=slot(src, p),
            dst_ref=slot(dst, p),
            send_sem=sems.at[0, p],
            recv_sem=sems.at[1, p],
            device_id=device,
            device_id_type=MESH,
        )

    def up_copy(p):
        return copy(up_out, up_in, up_sems, p, up_id)

    def side_copy(p):
        return copy(side_out, side_in, side_sems, p, right_id)

    def dside_copy(p):
        return copy(dside_out, dside_in, dside_sems, p, left_id)

    def down_copy(p):
        return copy(down_out, down_in, down_sems, p, down_id)

    def above_copy():
        return pltpu.make_async_remote_copy(
            src_ref=above_ref,
            dst_ref=above_side,
            send_sem=above_sems.at[0],
            recv_sem=above_sems.at[1],
            device_id=left_id,
            device_id_type=MESH,
        )

    first = s == 0

    @pl.when(first & has_left)
    def _():
        above_copy().start()

    @pl.when(jnp.logical_not(has_down))
    def _():
        up_in[...] = jnp.zeros_like(up_in)

    @pl.when(jnp.logical_not(has_left))
    def _():
        side_in[...] = jnp.zeros_like(side_in)

    @pl.when(jnp.logical_not(has_right))
    def _():
        dside_in[...] = jnp.zeros_like(dside_in)
        above_side[...] = jnp.zeros_like(above_side)

    spread = (
        lax.broadcasted_iota(jnp.int32, (blocks, features), 1) // size
        == lax.broadcasted_iota(jnp.int32, (blocks, features), 0)
    ).astype(jnp.bfloat16)
    factor_mask = dot_nn(pattern_ref[...].astype(jnp.float32).astype(jnp.bfloat16), spread)
    link_mask = dot_nn(coupling_pattern_ref[...].astype(jnp.float32).astype(jnp.bfloat16), spread)
    col_ids = lax.broadcasted_iota(jnp.int32, (size, features), 1)
    for i in range(blocks):
        part = pl.ds(i * size, size)
        row_ids = lax.broadcasted_iota(jnp.int32, (size, features), 0) + i * size
        keep = (factor_mask[i : i + 1, :] > 0.5) & (row_ids > col_ids)
        unit = jnp.where(row_ids == col_ids, 1.0, 0.0)
        factor[part, :] = jnp.where(keep, raw_ref[part, :].astype(jnp.float32), unit).astype(jnp.bfloat16)
        link[part, :] = jnp.where(
            link_mask[i : i + 1, :] > 0.5, coupling_ref[part, :].astype(jnp.float32), 0.0
        ).astype(jnp.bfloat16)

    tile = min(TILE, features)
    for m in range(0, features, tile):
        for n in range(0, features, tile):
            if m >= n:
                factor_t[n : n + tile, m : m + tile] = factor[m : m + tile, n : n + tile].T
            link_t[n : n + tile, m : m + tile] = link[m : m + tile, n : n + tile].T

    own_offset = offsets_ref[s, j]
    left_offset = offsets_ref[s, jnp.maximum(j - 1, 0)]
    child_offset = offsets_ref[jnp.minimum(s + 1, levels - 1), j]

    def forward(p):
        @pl.when(has_down)
        def _():
            up_copy(p).wait_recv()

        here = pl.ds(pl.multiple_of(p * rows, rows), rows)
        reduced = (given_ref[here, :] - up_in[here, :].astype(jnp.float32)).astype(jnp.bfloat16)
        result = jnp.concatenate(
            [
                dot_nn(reduced[:, : n + tile], factor_t[: n + tile, n : n + tile])
                for n in range(0, features, tile)
            ],
            axis=1,
        )
        kept[here, :] = result * pivot_ref[...]

        @pl.when(has_up)
        def _():
            side_out[here, :] = dot_nn(result.astype(jnp.bfloat16), link_t[...]).astype(jnp.bfloat16)

            @pl.when(has_right)
            def _():
                side_copy(p).start()

    def combine(p):
        @pl.when(has_up)
        def _():
            @pl.when(has_left)
            def _():
                side_copy(p).wait_recv()

            here = pl.ds(pl.multiple_of(p * rows, rows), rows)
            own = jnp.where(own_offset == 0, side_out[here, :].astype(jnp.float32), 0.0)
            moved = jnp.where(left_offset == 1, side_in[here, :].astype(jnp.float32), 0.0)
            up_out[here, :] = (own + jnp.where(has_left, moved, 0.0)).astype(jnp.bfloat16)
            up_copy(p).start()

    def backward(p):
        @pl.when(has_up)
        def _():
            down_copy(p).wait_recv()

        here = pl.ds(pl.multiple_of(p * rows, rows), rows)
        reduced = (kept[here, :] - dot_nn(down_in[here, :], link[...])).astype(jnp.bfloat16)
        result = jnp.concatenate(
            [dot_nn(reduced[:, n:], factor[n:, n : n + tile]) for n in range(0, features, tile)], axis=1
        )
        out_ref[here, :] = result

        @pl.when(has_down)
        def _():
            dside_out[here, :] = result.astype(jnp.bfloat16)

            @pl.when(has_left)
            def _():
                dside_copy(p).start()

    def select(p):
        @pl.when(has_down)
        def _():
            @pl.when(has_right)
            def _():
                dside_copy(p).wait_recv()

            here = pl.ds(pl.multiple_of(p * rows, rows), rows)
            down_out[here, :] = jnp.where(
                child_offset == 1,
                dside_in[here, :].astype(jnp.float32),
                dside_out[here, :].astype(jnp.float32),
            ).astype(jnp.bfloat16)
            down_copy(p).start()

    @pl.when(first)
    def _():
        @pl.when(has_right)
        def _():
            above_copy().wait_recv()

        down_in[...] = jnp.where(
            own_offset == 1, above_side[...].astype(jnp.float32), above_ref[...].astype(jnp.float32)
        ).astype(jnp.bfloat16)

    lag = jnp.minimum(LAG * s, pieces)

    def turn(u, carry):
        @pl.when(u < pieces)
        def _():
            forward(u)

        @pl.when((u >= 1) & (u <= pieces))
        def _():
            combine(u - 1)

        v = u - lag

        @pl.when((v >= 0) & (v < pieces))
        def _():
            backward(v)

        @pl.when((v >= 1) & (v <= pieces))
        def _():
            select(v - 1)

        return carry

    lax.fori_loop(0, pieces + lag + 1, turn, 0)

    def finish(p, carry):
        @pl.when(has_up)
        def _():
            up_copy(p).wait_send()

            @pl.when(has_right)
            def _():
                side_copy(p).wait_send()

        @pl.when(has_down)
        def _():
            down_copy(p).wait_send()

            @pl.when(has_left)
            def _():
                dside_copy(p).wait_send()

        return carry

    lax.fori_loop(0, pieces, finish, 0)

    @pl.when(first & has_left)
    def _():
        above_copy().wait_send()


def local(
    right_side,
    inverse_raw,
    inverse_pattern,
    coupling,
    coupling_pattern,
    pivots,
    offsets,
    above_solution,
):
    levels = lax.axis_size("section")
    nodes = lax.axis_size("scen")
    total, features = right_side.shape[2:]
    rows = min(ROWS, total)
    pieces = total // rows
    vmem = pl.BlockSpec(memory_space=pltpu.VMEM)
    half = pltpu.VMEM((total, features), jnp.bfloat16)
    square = pltpu.VMEM((features, features), jnp.bfloat16)
    sems = pltpu.SemaphoreType.DMA((2, pieces))
    solved = pl.pallas_call(
        functools.partial(kernel, levels, nodes, rows),
        out_shape=pltpu.VMEM((total, features), jnp.float32),
        in_specs=[vmem] * 6 + [pl.BlockSpec(memory_space=pltpu.SMEM), vmem],
        out_specs=vmem,
        scratch_shapes=[square] * 4 + [pltpu.VMEM((total, features), jnp.float32)]
        + [half] * 9
        + [sems] * 4
        + [pltpu.SemaphoreType.DMA((2,))],
        compiler_params=pltpu.CompilerParams(
            collective_id=0, has_side_effects=True, vmem_limit_bytes=60 * 1024 * 1024
        ),
    )(
        right_side[0, 0],
        inverse_raw[0, 0],
        inverse_pattern[0, 0],
        coupling[0, 0],
        coupling_pattern[0, 0],
        pivots[0],
        offsets,
        above_solution[0],
    )
    return solved[None, None]


def solution(mesh):
    placed = (
        P("section", "scen", None, None),
        P("section", "scen", None, None),
        P("section", "scen", None, None),
        P("section", "scen", None, None),
        P("section", "scen", None, None),
        P("section", "scen", None),
        P(),
        P("scen", None, None),
    )
    return jax.shard_map(
        local,
        mesh=mesh,
        in_specs=placed,
        out_specs=P("section", "scen", None, None),
        check_vma=False,
    )
```
